32 devices in a mesh: row: 4 (over x, core), col: 8 (over z, y).
Axes of the slice: x: 2, y: 2, z: 4, core: 2. Of those that a mesh axis runs over, the one named last changes fastest.
Arguments:
- pre_act: bfloat16 [3072, 4096], P('col'), may hold values from -6 to 6
- grad_out: bfloat16 [3072, 4096], P('col', 'row'), may hold values from -6 to 6
- w_down: bfloat16 [4096, 4096], P('col', 'row'), may hold values from -0.09375 to 0.09375
Outputs:
- w_grad: float32 [4096, 4096], P('col', 'row')
- grad_pre: bfloat16 [3072, 4096], P('col', 'row')
The draws below stay inside these ranges and needn't reach their ends.
All inputs are finite; a program needn't handle non-finite values.
Results may differ from the reference program's by a relative error of at most 0.0095.
Values may be sent and summed in bfloat16 or wider, within the bound.
No kernel may reach another device: no remote copies, remote signals or barrier semaphores. Data moves between devices by JAX's collectives and lax.ppermute only.
A program may use at most 128 MiB of HBM per device.

```python
import jax
import jax.numpy as jnp
from jax import lax

D = 4096
FF = 4096
TOKENS = 3072
N_ROW = 4


def raised(values, key, source, target, shards_of, factor):
    owner, partner = [(jnp.arange(values.shape[axis_at]) // (values.shape[axis_at] // shards_of)).reshape([-1 if axis == axis_at else 1 for axis in range(values.ndim)]) for axis_at in (source, target)]
    chosen = jax.random.permutation(key, shards_of)[partner]
    strong = (owner == chosen) | (owner == (partner + shards_of // 2) % shards_of)
    return jnp.where(strong, factor * values, values)


def block_scale(own_key, extent, split, low, largest):
    gain, own = 1.0, jax.random.fold_in(own_key, 6)
    for dim, shards_of in split:
        steps = jnp.exp(jax.random.uniform(jax.random.fold_in(own, dim), (shards_of,), jnp.float32, low / len(split), largest / len(split)))
        gain = gain * jnp.repeat(steps, extent[dim] // shards_of).reshape([-1 if axis == dim else 1 for axis in range(len(extent))])
    return gain


def scatter_about(stream_key, extent, scale, limit, cuts=(), kind=jnp.bfloat16):
    result = jax.random.normal(stream_key, extent, jnp.float32) * scale
    if len(cuts) > 0:
        result = block_scale(stream_key, extent, cuts, -0.22, 0.18) * result
    return jnp.clip(result, min=-limit, max=limit).astype(kind)


def gaussian_with(key, dims, width, most, split, heavy, kind=jnp.bfloat16):
    values = width * jax.random.normal(key, dims, jnp.float32)
    if split:
        values = values * block_scale(key, dims, split, -0.22, 0.18)
    return jnp.clip(raised(values, jax.random.fold_in(key, 3), *heavy), -most, most).astype(kind)


def setup_inputs(seed: int = 0) -> dict:
    arg_keys = jax.random.split(jax.random.key(seed), 4)
    pre_act = gaussian_with(arg_keys[0], (TOKENS, FF), 1.0, 6.0, ((0, 8),), (0, 1, 8, 2.0))
    grad_out = scatter_about(arg_keys[1], (TOKENS, D), 1.0, 6.0, ((0, 8), (1, 4)))
    w_down = scatter_about(arg_keys[2], (FF, D), FF ** -0.5, 0.09375, ((0, 8), (1, 4)))
    return dict(pre_act=pre_act, grad_out=grad_out, w_down=w_down)


def reference(pre_act, grad_out, w_down):
    hidden = jnp.maximum(pre_act, jnp.zeros((), jnp.bfloat16)).astype(jnp.bfloat16)
    scale = 1.0 / jnp.sqrt(jnp.float32(TOKENS))
    product = lax.dot_general(hidden, grad_out, (((0,), (0,)), ((), ())), preferred_element_type=jnp.float32)
    w_grad = product * scale
    block = D // N_ROW
    total = jnp.zeros((pre_act.shape[0], FF), jnp.float32)
    for quarter in range(N_ROW):
        left = grad_out[:, quarter * block:(quarter + 1) * block]
        right = w_down[:, quarter * block:(quarter + 1) * block]
        partial_sum = lax.dot_general(left, right, (((1,), (1,)), ((), ())), preferred_element_type=jnp.float32)
        rounded = lax.optimization_barrier(partial_sum.astype(jnp.bfloat16))
        total = total + rounded.astype(jnp.float32)
    grad_pre = jnp.where(pre_act > 0, total, jnp.zeros((), jnp.float32)).astype(jnp.bfloat16)
    return (w_grad, grad_pre)
```

```python
import jax
import jax.numpy as jnp
from jax import lax
from jax.sharding import PartitionSpec as P


BF16 = jnp.bfloat16
F32 = jnp.float32


def dot_rows(a, b):
    return lax.dot_general(a, b, (((0,), (0,)), ((), ())), preferred_element_type=F32)


def dot_features(a, b):
    return lax.dot_general(a, b, (((1,), (1,)), ((), ())), preferred_element_type=F32)


def any_mesh(pre_act, grad_out, w_down):
    hidden = jnp.maximum(pre_act, jnp.zeros((), BF16))
    col_count = lax.axis_size("col")
    row_count = lax.axis_size("row")
    scale = 1.0 / jnp.sqrt(F32(hidden.shape[0] * col_count))
    quarter = hidden.shape[1] // row_count
    hidden_part = lax.all_to_all(hidden, "col", split_axis=1, concat_axis=0, tiled=True)
    piece = lax.all_gather(grad_out, "col", axis=0, tiled=True)
    w_grad = dot_rows(hidden_part, piece) * scale
    partial = dot_features(piece, w_down).astype(BF16)
    returned = lax.all_to_all(partial, "col", split_axis=0, concat_axis=1, tiled=True)
    summed = lax.psum(returned, "row").astype(F32)
    offset = lax.axis_index("row") * quarter
    own_sum = lax.dynamic_slice_in_dim(summed, offset, quarter, 1)
    own_pre = lax.dynamic_slice_in_dim(pre_act, offset, quarter, 1)
    grad_pre = jnp.where(own_pre > 0, own_sum, F32(0)).astype(BF16)
    return (w_grad, grad_pre)


def line_of_pairs(pre_act, grad_out, w_down):
    rows, cols = lax.axis_size("row"), lax.axis_size("col")
    zs = cols // 2
    tokens, units = pre_act.shape
    features = grad_out.shape[1]
    unit_half = w_down.shape[0]
    unit_block = 2 * unit_half
    quarter = tokens // rows
    scale = 1.0 / jnp.sqrt(F32(tokens * cols))

    r, c = lax.axis_index("row"), lax.axis_index("col")
    x, k, z, y = r // 2, r % 2, c // 2, c % 2
    own_quarter = 2 * k + x

    def move(value, route):
        pairs = []
        for source in range(rows * cols):
            sr, sc = divmod(source, cols)
            target = route(sr // 2, sr % 2, sc // 2, sc % 2)
            if target is not None:
                tx, tk, tz, ty = target
                pairs.append((source, (2 * tx + tk) * cols + 2 * tz + ty))
        return lax.ppermute(value, ("row", "col"), pairs)

    def over_z(s):
        return lambda x, k, z, y: (x, k, z ^ s, y)

    def middle(x, k, z, y):
        return (x, k, zs - 1 - z, y) if 0 < z < zs - 1 else None

    def outward(x, k, z, y):
        return (x, k, z ^ 1, y) if 0 < z < zs - 1 else None

    def over_x(x, k, z, y):
        return (1 - x, k, z, y)

    def over_k(x, k, z, y):
        return (x, 1 - k, z, y)

    def over_y(x, k, z, y):
        return (x, k, z, 1 - y)

    def relative(value):
        parts = value.reshape((2, 2, quarter) + value.shape[1:])
        parts = jnp.where(k == 0, parts, parts[::-1])
        parts = jnp.where(x == 0, parts, parts[:, ::-1])
        return parts.reshape(value.shape)

    g0 = relative(grad_out)
    w_other = move(w_down, over_y)
    near = move(g0, over_z(1))
    mid1 = move(g0, middle)
    mid2 = move(near, middle)
    end1 = move(mid1, outward)
    end2 = move(mid2, outward)
    g = [g0, near, end1 + mid2, end2 + mid1]

    def unit_slice(s):
        base = (z ^ s) * unit_block
        half = [
            lax.dynamic_slice(pre_act, (own_quarter * quarter, base + (y ^ i) * unit_half), (quarter, unit_half))
            for i in (0, 1)
        ]
        return jnp.maximum(jnp.stack(half), jnp.zeros((), BF16))

    arrived = jnp.stack([move(unit_slice(s), over_z(s)) for s in range(1, zs)], 1)
    both_x = jnp.stack([arrived, move(arrived, over_x)], 2)
    joined = jnp.concatenate([both_x, move(both_x, over_k)], 2)
    joined = joined.reshape(2, zs - 1, tokens, unit_half)

    def own_units(i):
        part = lax.dynamic_slice(pre_act, (0, z * unit_block + (y ^ i) * unit_half), (tokens, unit_half))
        return relative(jnp.maximum(part, jnp.zeros((), BF16)))

    w_pair = jnp.where(
        y == 0, jnp.concatenate([w_down, w_other]), jnp.concatenate([w_other, w_down])
    )
    home = [jnp.zeros((quarter, unit_block), BF16)] * rows
    for s in range(zs):
        partial = dot_features(g[s], w_pair).astype(BF16)
        half = partial[: 2 * quarter].astype(F32) + move(partial[2 * quarter :], over_k).astype(F32)
        total = half[:quarter] + move(half[quarter:].astype(BF16), over_x).astype(F32)
        total = total.astype(BF16)
        for sender in range(rows):

            def homeward(x, k, z, y):
                return (z // 2, z % 2, z ^ s, y) if 2 * x + k == sender else None

            place = 2 * (sender % 2) + sender // 2
            home[place] = home[place] + move(total, homeward)
    own_sum = jnp.concatenate(home)
    own_pre = lax.dynamic_slice_in_dim(pre_act, r * unit_block, unit_block, 1)
    grad_pre = jnp.where(own_pre > 0, own_sum, jnp.zeros((), BF16))

    def gradient(i):
        total = dot_rows(own_units(i), g[0])
        for s in range(1, zs):
            total = total + dot_rows(joined[i, s - 1], g[s])
        return total

    other = move(gradient(1).astype(BF16), over_y)
    w_grad = (gradient(0) + other.astype(F32)) * scale
    return (w_grad, grad_pre)


def solution(mesh):
    rows, cols = mesh.shape["row"], mesh.shape["col"]
    line = rows == 4 and cols == 2 * rows
    placed = (P("col", None), P("col", "row"), P("col", "row"))
    return jax.shard_map(
        line_of_pairs if line else any_mesh,
        mesh=mesh,
        in_specs=placed,
        out_specs=(P("col", "row"), P("col", "row")),
        check_vma=False,
    )
```
